256 devices in a mesh: sec: 2 (over core), blk: 128 (over y, x, z).
Axes of the slice: x: 4, y: 4, z: 8, core: 2. Of those that a mesh axis runs over, the one named last changes fastest.
Arguments:
- columns: bfloat16 [2, 128, 8, 128, 2048], P('sec', 'blk'), may hold values from -6 to 6
- mixing: bfloat16 [2, 128, 128, 128], P('sec', 'blk'), may hold values from -0.5 to 0.5
- lagged_flux: bfloat16 [128, 8, 2048], P('blk'), may hold values from -6 to 6
- coefficients: float32 [8], replicated, may hold values from 0.5 to 2
- ocean_mask: int32 [128, 2048], P('blk'), may hold values 0 or 1
- atm_tile: int32 [128, 5, 16], P('blk'), may hold values from 0 to 15
- ocean_tile: int32 [128, 5, 16], P('blk'), may hold values from 0 to 15
- live: int32 [128, 5, 16], P('blk'), may hold values from 0 to 1, as said below
- weights: bfloat16 [128, 5, 16, 128, 128], P('blk'), may hold values from -0.5 to 0.5
Outputs:
- new_columns: bfloat16 [2, 128, 8, 128, 2048], P('sec', 'blk')
- flux_out: bfloat16 [2, 128, 8, 2048], P('sec', 'blk')
The draws below stay inside these ranges and needn't reach their ends.
Inputs may be any that keep to these rules, and one draw needn't show every extreme that they name: The share of live slots differs from block to block.
All inputs are finite; a program needn't handle non-finite values. No bound on the sum of `ocean_mask` on one device may be relied on, other than what follows from the above.
Results may differ from the reference program's by a relative error of at most 0.0062.
Values may be sent and summed in bfloat16 or wider, within the bound.
No kernel may reach another device: no remote copies, remote signals or barrier semaphores. Data moves between devices by JAX's collectives and lax.ppermute only.
A program may use at most 128 MiB of HBM per device.

```python
import math
import jax
import jax.numpy as jnp
from jax import lax

FLD = 8
LEV = 128
TILE = 128
C = 2048
REACH = 2
SLOTS = 16
NT = 16
P_SIZE = 5
NB = 128


def draw_live(key, part):
    first_key, second_key = jax.random.split(jax.random.fold_in(key, 7))
    share = jax.random.randint(first_key, (NB, 1, 1), 1, 17)
    roll = jax.random.randint(second_key, (NB, P_SIZE, SLOTS), 0, 16)
    return (roll < share).astype(jnp.int32)


def with_ends(array, key, low, largest):
    dims = array.shape
    place = [jax.random.randint(jax.random.fold_in(key, axis), (), 0, dims[axis]) for axis in range(len(dims))]
    array = array.at[tuple(place)].set(low)
    longest = dims.index(max(dims))
    place[longest] = (place[longest] + 1) % dims[longest]
    return array.at[tuple(place)].set(largest)


def steps_of(stream_key, dims, pieces, smallest, high):
    def one(axis_at, shards_of):
        draws = jax.random.uniform(jax.random.fold_in(jax.random.fold_in(stream_key, 6), axis_at), (shards_of,), jnp.float32, smallest / len(pieces), high / len(pieces))
        return jnp.repeat(jnp.exp(draws), dims[axis_at] // shards_of).reshape((-1,) + (1,) * (len(dims) - axis_at - 1))

    factor_of = one(*pieces[0])
    for cut in pieces[1:]:
        factor_of = factor_of * one(*cut)
    return factor_of


def normal_values(key, shape, deviation, limit, pieces=(), kind=jnp.bfloat16):
    entries = jax.random.normal(key, shape, jnp.float32) * deviation
    if len(pieces) > 0:
        entries = steps_of(key, shape, pieces, -0.22, 0.18) * entries
    return jnp.clip(entries, min=-limit, max=limit).astype(kind)


def setup_inputs(seed: int = 0) -> dict:
    splits = jax.random.split(jax.random.key(seed), 10)
    columns = normal_values(splits[0], (2, NB, FLD, LEV, C), 1.0, 6.0, ((0, 2), (1, 128)))
    mixing = normal_values(splits[1], (2, NB, LEV, LEV), LEV ** -0.5, 0.5, ((0, 2), (1, 128)))
    lagged_flux = normal_values(splits[2], (NB, FLD, C), 1.0, 6.0, ((0, 128),))
    coefficients = jnp.clip(jnp.exp(jax.random.uniform(splits[3], (FLD,), jnp.float32, math.log(0.5), math.log(2.0))), 0.5, 2.0)
    ocean_mask = with_ends((jax.random.randint(splits[4], (NB, C), 0, 4) < 3).astype(jnp.int32), jax.random.fold_in(splits[4], 1), 0, 1)
    atm_tile = with_ends(jax.random.randint(splits[5], (NB, P_SIZE, SLOTS), 0, NT), jax.random.fold_in(splits[5], 1), 0, NT - 1).astype(jnp.int32)
    ocean_tile = with_ends(jax.random.randint(splits[6], (NB, P_SIZE, SLOTS), 0, NT), jax.random.fold_in(splits[6], 1), 0, NT - 1).astype(jnp.int32)
    live = draw_live(jax.random.fold_in(splits[9], 71), 0)
    weights = normal_values(splits[8], (NB, P_SIZE, SLOTS, TILE, TILE), TILE ** -0.5, 0.5, ((0, 128),))
    return {"columns": columns, "mixing": mixing, "lagged_flux": lagged_flux, "coefficients": coefficients, "ocean_mask": ocean_mask, "atm_tile": atm_tile, "ocean_tile": ocean_tile, "live": live, "weights": weights}


step_weight = 0.25

def mix_block(pair):
    column_data, mixing_block = pair
    wide = column_data.astype(jnp.float32)
    mixed = wide + jnp.einsum('kl,flc->fkc', mixing_block.astype(jnp.float32), wide)
    return (mixed.astype(jnp.bfloat16), mixed[:, 0, :])

def forward_block(args):
    surface_tiles, tile_number, live_block, weight_block = args
    picked = surface_tiles[tile_number].astype(jnp.float32)
    product = jnp.einsum('psfi,psij->psfj', picked, weight_block.astype(jnp.float32))
    return (product * live_block[:, :, None, None].astype(jnp.float32)).astype(jnp.bfloat16)

def backward_block(args):
    flux_tiles, weight_block = args
    return jnp.einsum('psfj,psij->psfi', flux_tiles.astype(jnp.float32), weight_block.astype(jnp.float32))

def reference(columns, mixing, lagged_flux, coefficients, ocean_mask, atm_tile, ocean_tile, live, weights):
    rounded, level_zero = lax.map(mix_block, (columns.reshape(2 * NB, FLD, LEV, C), mixing.reshape(2 * NB, LEV, LEV)))
    atm_surface = (level_zero[:NB] - step_weight * lagged_flux.astype(jnp.float32)).astype(jnp.bfloat16)
    ocean_level = level_zero[NB:]
    surface_tiles = atm_surface.reshape(NB, FLD, NT, TILE).transpose(0, 2, 1, 3)
    contrib = lax.map(forward_block, (surface_tiles, atm_tile, live, weights))
    dest_block = jnp.arange(NB, dtype=jnp.int32)[:, None] + jnp.arange(P_SIZE, dtype=jnp.int32)[None, :] - REACH
    inside = (dest_block >= 0) & (dest_block < NB)
    valid = inside[:, :, None] & (live == 1)
    segment = jnp.where(valid, dest_block[:, :, None] * NT + ocean_tile, NB * NT)
    summed = jax.ops.segment_sum(contrib.reshape(NB * P_SIZE * SLOTS, FLD, TILE).astype(jnp.float32), segment.reshape(-1), num_segments=NB * NT + 1)
    remapped = summed[:NB * NT].reshape(NB, NT, FLD, TILE).transpose(0, 2, 1, 3).reshape(NB, FLD, C)
    across = remapped[:, 0] - ocean_level[:, 0]
    along = remapped[:, 1] - ocean_level[:, 1]
    speed = jnp.sqrt(across * across + along * along + 1.0)
    ocean_flux = (coefficients[None, :, None] * speed[:, None, :] * (remapped - ocean_level) * ocean_mask[:, None, :].astype(jnp.float32)).astype(jnp.bfloat16)
    flux_tiles = ocean_flux.reshape(NB, FLD, NT, TILE).transpose(0, 2, 1, 3)
    clipped = jnp.clip(dest_block, 0, NB - 1)
    returned = flux_tiles[clipped[:, :, None], ocean_tile] * valid[:, :, :, None, None].astype(jnp.bfloat16)
    back = lax.map(backward_block, (returned, weights))
    atm_segment = jnp.arange(NB, dtype=jnp.int32)[:, None, None] * NT + atm_tile
    atm_sum = jax.ops.segment_sum(back.reshape(NB * P_SIZE * SLOTS, FLD, TILE), atm_segment.reshape(-1), num_segments=NB * NT)
    atm_flux = atm_sum.reshape(NB, NT, FLD, TILE).transpose(0, 2, 1, 3).reshape(NB, FLD, C).astype(jnp.bfloat16)
    ocean_top = (ocean_level + step_weight * ocean_flux.astype(jnp.float32)).astype(jnp.bfloat16)
    top_level = jnp.concatenate([atm_surface, ocean_top], axis=0)
    new_columns = rounded.at[:, :, 0, :].set(top_level).reshape(2, NB, FLD, LEV, C)
    flux_out = jnp.stack([atm_flux, ocean_flux], axis=0)
    return (new_columns, flux_out)
```

```python
import jax
import jax.numpy as jnp
import numpy as np
from jax import lax
from jax.experimental import pallas as pl
from jax.experimental.pallas import tpu as pltpu
from jax.sharding import PartitionSpec as P

step_weight = 0.25
axes = ("sec", "blk")
VMEM = pl.BlockSpec(memory_space=pltpu.VMEM)
SMEM = pl.BlockSpec(memory_space=pltpu.SMEM)
ANY = pl.BlockSpec(memory_space=pl.ANY)


def partner(block, distance, phase, count):
    other = block + distance if (block // distance) % 2 == phase else block - distance
    return other if 0 <= other < count else block


def exchange_pairs(count, phase):
    first = [(b, partner(b, 2, phase, count)) for b in range(count)]
    second = [(count + b, count + partner(b, 1, phase, count)) for b in range(count)]
    return first + second


def swap_pairs(count):
    return [(b, count + b) for b in range(count)] + [(count + b, b) for b in range(count)]


def level_kernel(meta, columns, mixing, lagged, out, buffer, semaphore):
    fields = buffer.shape[0]
    copies = [
        pltpu.make_async_copy(columns.at[0, 0, f], buffer.at[f], semaphore.at[f])
        for f in range(fields)
    ]
    for copy in copies:
        copy.start()
    rows = mixing[0, 0, 0:16, :]
    for f in range(fields):
        copies[f].wait()
        product = jnp.dot(rows, buffer[f], preferred_element_type=jnp.float32)
        level = product + buffer[f, 0:16, :].astype(jnp.float32)
        out[f : f + 1, :] = level[0:1, :]

    @pl.when(meta[0] == 0)
    def _():
        surface = out[...] - step_weight * lagged[0].astype(jnp.float32)
        out[...] = surface.astype(jnp.bfloat16).astype(jnp.float32)


def remap_kernel(meta, atm_tile, ocean_tile, live, surface, weights, first, second, own, tiles, sums):
    count, fields, width = tiles.shape
    for t in range(count):
        tiles[t] = surface[:, t * width : (t + 1) * width]
    sums[...] = jnp.zeros_like(sums)
    slots = live.shape[2]
    half = slots // 2
    jobs = [(g, k) for k in range(slots) for g in (0, 1)]
    jobs += [(2, k) for k in range(half)]
    for g, k in jobs:
        p = meta[1 + g]
        slot = k if g < 2 else k + meta[0] * half
        part = tiles[atm_tile[0, p, slot]].astype(jnp.bfloat16)
        product = jnp.dot(part, weights[0, p, slot], preferred_element_type=jnp.float32)
        product = product.astype(jnp.bfloat16).astype(jnp.float32)
        target = ocean_tile[0, p, slot]
        keep = live[0, p, slot] == 1
        sums[g, target] = sums[g, target] + jnp.where(keep, product, 0.0)
    for t in range(count):
        span = slice(t * width, (t + 1) * width)
        first[:, span] = sums[0, t].astype(jnp.bfloat16)
        second[:, span] = sums[1, t].astype(jnp.bfloat16)
        own[:, span] = sums[2, t]


def back_kernel(meta, atm_tile, ocean_tile, live, first, second, own, weights, out, tiles, sums):
    _, count, fields, width = tiles.shape
    for t in range(count):
        span = slice(t * width, (t + 1) * width)
        tiles[0, t] = first[:, span].astype(jnp.float32)
        tiles[1, t] = second[:, span].astype(jnp.float32)
        tiles[2, t] = own[:, span].astype(jnp.float32)
    sums[...] = jnp.zeros_like(sums)
    slots = live.shape[2]
    half = slots // 2
    jobs = [(g, k) for k in range(slots) for g in (0, 1)]
    jobs += [(2, k) for k in range(half)]
    for i, (g, k) in enumerate(jobs):
        p = meta[1 + g]
        slot = k if g < 2 else k + meta[0] * half
        part = tiles[g, ocean_tile[0, p, slot]].astype(jnp.bfloat16)
        product = lax.dot_general(
            part,
            weights[0, p, slot],
            (((1,), (1,)), ((), ())),
            preferred_element_type=jnp.float32,
        )
        target = atm_tile[0, p, slot]
        keep = live[0, p, slot] * meta[4 + g] == 1
        sums[i % 2, target] = sums[i % 2, target] + jnp.where(keep, product, 0.0)
    for t in range(count):
        out[:, t * width : (t + 1) * width] = sums[0, t] + sums[1, t]


def mix_kernel(columns, mixing, top, out):
    field = pl.program_id(0)
    column = columns[0, 0, 0]
    mixed = column.astype(jnp.float32) + jnp.dot(
        mixing[0, 0], column, preferred_element_type=jnp.float32
    )
    out[0, 0, 0] = mixed.astype(jnp.bfloat16)
    row = lax.broadcasted_iota(jnp.int32, (16, column.shape[1]), 0)
    above = jnp.broadcast_to(top[pl.ds(field, 1), :], (16, column.shape[1]))
    out[0, 0, 0, 0:16, :] = jnp.where(row == 0, above, mixed[0:16, :]).astype(jnp.bfloat16)


def local(
    columns, mixing, lagged_flux, coefficients, ocean_mask, atm_tile, ocean_tile, live, weights
):
    _, _, fields, levels, cells = columns.shape
    width = weights.shape[3]
    tiles = cells // width
    count = lax.axis_size("blk")
    sec = lax.axis_index("sec")
    blk = lax.axis_index("blk")
    table = np.zeros((2, count, 8), np.int32)
    for core in (0, 1):
        for b in range(count):
            others = [partner(b, 2 - core, phase, count) for phase in (1, 0)]
            table[core, b, 0] = core
            table[core, b, 1:3] = [other - b + 2 for other in others]
            table[core, b, 3] = 2
            table[core, b, 4:6] = [other != b for other in others]
            table[core, b, 6] = 1
    meta = lax.dynamic_slice(jnp.asarray(table), (sec, blk, 0), (1, 1, 8)).reshape(8)
    swap = swap_pairs(count)
    wide = exchange_pairs(count, 1)
    near = exchange_pairs(count, 0)
    field_f32 = jax.ShapeDtypeStruct((fields, cells), jnp.float32)
    field_bf16 = jax.ShapeDtypeStruct((fields, cells), jnp.bfloat16)

    level = pl.pallas_call(
        level_kernel,
        out_shape=field_f32,
        in_specs=[SMEM, ANY, VMEM, VMEM],
        out_specs=VMEM,
        scratch_shapes=[
            pltpu.VMEM((fields, levels, cells), jnp.bfloat16),
            pltpu.SemaphoreType.DMA((fields,)),
        ],
        compiler_params=pltpu.CompilerParams(vmem_limit_bytes=24 << 20),
    )(meta, columns, mixing, lagged_flux)
    other_level = lax.ppermute(level, axes, swap)
    is_atm = sec == 0
    surface = jnp.where(is_atm, level, other_level)
    ocean_level = jnp.where(is_atm, other_level, level)

    first, second, own = pl.pallas_call(
        remap_kernel,
        out_shape=(field_bf16, field_bf16, field_f32),
        in_specs=[SMEM, SMEM, SMEM, SMEM, VMEM, VMEM],
        out_specs=(VMEM, VMEM, VMEM),
        scratch_shapes=[
            pltpu.VMEM((tiles, fields, width), jnp.float32),
            pltpu.VMEM((3, tiles, fields, width), jnp.float32),
        ],
        compiler_params=pltpu.CompilerParams(vmem_limit_bytes=24 << 20),
    )(meta, atm_tile, ocean_tile, live, surface, weights)
    got_first = lax.ppermute(first, axes, wide)
    got_second = lax.ppermute(second, axes, near)
    partial = (
        own
        + jnp.where(meta[4] == 1, got_first.astype(jnp.float32), 0.0)
        + jnp.where(meta[5] == 1, got_second.astype(jnp.float32), 0.0)
    )
    remapped = partial + lax.ppermute(partial, axes, swap)

    difference = remapped - ocean_level
    speed = jnp.sqrt(
        difference[0:1] * difference[0:1] + difference[1:2] * difference[1:2] + 1.0
    )
    ocean_flux = (
        coefficients[:, None] * speed * difference * ocean_mask.astype(jnp.float32)
    ).astype(jnp.bfloat16)
    top = jnp.where(
        is_atm, surface, ocean_level + step_weight * ocean_flux.astype(jnp.float32)
    )

    flux_first = lax.ppermute(ocean_flux, axes, wide)
    flux_second = lax.ppermute(ocean_flux, axes, near)

    block = (1, 1, 1, levels, cells)
    new_columns = pl.pallas_call(
        mix_kernel,
        grid=(fields,),
        out_shape=jax.ShapeDtypeStruct(columns.shape, jnp.bfloat16),
        in_specs=[
            pl.BlockSpec(block, lambda f: (0, 0, f, 0, 0)),
            pl.BlockSpec((1, 1, levels, levels), lambda f: (0, 0, 0, 0)),
            pl.BlockSpec((fields, cells), lambda f: (0, 0)),
        ],
        out_specs=pl.BlockSpec(block, lambda f: (0, 0, f, 0, 0)),
        cost_estimate=pl.CostEstimate(
            flops=2 * fields * levels * levels * cells,
            transcendentals=0,
            bytes_accessed=4 * fields * levels * cells,
        ),
        compiler_params=pltpu.CompilerParams(vmem_limit_bytes=24 << 20),
    )(columns, mixing, top)

    half = pl.pallas_call(
        back_kernel,
        out_shape=field_f32,
        in_specs=[SMEM, SMEM, SMEM, SMEM, VMEM, VMEM, VMEM, VMEM],
        out_specs=VMEM,
        scratch_shapes=[
            pltpu.VMEM((3, tiles, fields, width), jnp.float32),
            pltpu.VMEM((2, tiles, fields, width), jnp.float32),
        ],
        compiler_params=pltpu.CompilerParams(vmem_limit_bytes=24 << 20),
    )(meta, atm_tile, ocean_tile, live, flux_first, flux_second, ocean_flux, weights)
    atm_flux = (half + lax.ppermute(half, axes, swap)).astype(jnp.bfloat16)
    flux_here = jnp.where(is_atm, atm_flux, ocean_flux)
    return (new_columns, flux_here[None, None])


def solution(mesh):
    in_specs = (
        P("sec", "blk", None, None, None),
        P("sec", "blk", None, None),
        P("blk", None, None),
        P(),
        P("blk", None),
        P("blk", None, None),
        P("blk", None, None),
        P("blk", None, None),
        P("blk", None, None, None, None),
    )
    out_specs = (P("sec", "blk", None, None, None), P("sec", "blk", None, None))
    return jax.shard_map(local, mesh=mesh, in_specs=in_specs, out_specs=out_specs, check_vma=False)
```

```python
import jax
import jax.numpy as jnp
from jax import lax
from jax.experimental import pallas as pl
from jax.experimental.pallas import tpu as pltpu
from jax.sharding import PartitionSpec as P

step_weight = 0.25
axes = ("sec", "blk")
VMEM = pl.BlockSpec(memory_space=pltpu.VMEM)
SMEM = pl.BlockSpec(memory_space=pltpu.SMEM)
ANY = pl.BlockSpec(memory_space=pl.ANY)
HBM = pl.BlockSpec(memory_space=pltpu.HBM)


def partner(block, distance, phase, count):
    other = block + distance if (block // distance) % 2 == phase else block - distance
    return other if 0 <= other < count else block


def exchange_pairs(count, phase):
    first = [(b, partner(b, 2, phase, count)) for b in range(count)]
    second = [(count + b, count + partner(b, 1, phase, count)) for b in range(count)]
    return first + second


def swap_pairs(count):
    return [(b, count + b) for b in range(count)] + [(count + b, b) for b in range(count)]


def place():
    count = lax.axis_size("blk")
    core = lax.axis_index("sec")
    block = lax.axis_index("blk")
    reach = 2 - core
    shift = 1 - core
    place_in_pair = jnp.bitwise_and(lax.shift_right_logical(block, shift), 1)
    wide_step = jnp.where(place_in_pair == 1, reach, -reach)
    near_step = -wide_step
    found = []
    for step in (wide_step, near_step):
        other = block + step
        found.append(jnp.logical_and(other >= 0, other < count))
    return core, (wide_step + 2, near_step + 2), found


def level_kernel(columns, mixing, lagged, out, buffer, rows, late, semaphore, extra):
    fields = buffer.shape[0]
    small = [
        pltpu.make_async_copy(mixing.at[0, 0, 0:16], rows, extra.at[0]),
        pltpu.make_async_copy(lagged.at[0], late, extra.at[1]),
    ]
    copies = [
        pltpu.make_async_copy(columns.at[0, 0, f], buffer.at[f], semaphore.at[f])
        for f in range(fields)
    ]
    small[0].start()
    for copy in copies:
        copy.start()
    small[1].start()
    small[0].wait()
    for f in range(fields):
        copies[f].wait()
        product = jnp.dot(rows[...], buffer[f], preferred_element_type=jnp.float32)
        level = product + buffer[f, 0:16, :].astype(jnp.float32)
        out[f : f + 1, :] = level[0:1, :]
    small[1].wait()

    @pl.when(lax.axis_index("sec") == 0)
    def _():
        surface = out[...] - step_weight * late[...].astype(jnp.float32)
        out[...] = surface.astype(jnp.bfloat16).astype(jnp.float32)


def slot_jobs(core, distances, slots):
    half = slots // 2
    jobs = [(g, distances[g], k) for k in range(slots) for g in (0, 1)]
    return jobs + [(2, 2, k + core * half) for k in range(half)]


def remap_kernel(codes, surface, weights, first, second, own, tiles, sums):
    count, fields, width = tiles.shape
    core, distances, _ = place()
    for t in range(count):
        tiles[t] = surface[:, t * width : (t + 1) * width]
    sums[...] = jnp.zeros_like(sums)
    for g, p, slot in slot_jobs(core, distances, weights.shape[2]):
        code = codes[0, p, slot]
        part = tiles[jnp.bitwise_and(code, 255)].astype(jnp.bfloat16)
        product = jnp.dot(part, weights[0, p, slot], preferred_element_type=jnp.float32)
        product = product.astype(jnp.bfloat16).astype(jnp.float32)
        target = jnp.bitwise_and(lax.shift_right_logical(code, 8), 255)
        keep = lax.shift_right_logical(code, 16) == 1
        sums[g, target] = sums[g, target] + jnp.where(keep, product, 0.0)
    for t in range(count):
        span = slice(t * width, (t + 1) * width)
        first[:, span] = sums[0, t].astype(jnp.bfloat16)
        second[:, span] = sums[1, t].astype(jnp.bfloat16)
        own[:, span] = sums[2, t]


def back_kernel(codes, second, first, own, weights, after, out, tiles, sums):
    del after
    _, count, fields, width = tiles.shape
    core, distances, found = place()
    for t in range(count):
        span = slice(t * width, (t + 1) * width)
        tiles[0, t] = first[:, span].astype(jnp.float32)
        tiles[1, t] = second[:, span].astype(jnp.float32)
        tiles[2, t] = own[:, span].astype(jnp.float32)
    sums[...] = jnp.zeros_like(sums)
    for i, (g, p, slot) in enumerate(slot_jobs(core, distances, weights.shape[2])):
        code = codes[0, p, slot]
        source = jnp.bitwise_and(lax.shift_right_logical(code, 8), 255)
        part = tiles[g, source].astype(jnp.bfloat16)
        product = lax.dot_general(
            part,
            weights[0, p, slot],
            (((1,), (1,)), ((), ())),
            preferred_element_type=jnp.float32,
        )
        target = jnp.bitwise_and(code, 255)
        keep = lax.shift_right_logical(code, 16) == 1
        if g < 2:
            keep = jnp.logical_and(keep, found[g])
        sums[i % 2, target] = sums[i % 2, target] + jnp.where(keep, product, 0.0)
    for t in range(count):
        out[:, t * width : (t + 1) * width] = sums[0, t] + sums[1, t]


def mix_kernel(columns, mixing, top, out, done):
    done[...] = jnp.zeros_like(done)
    field = pl.program_id(0)
    column = columns[0, 0, 0]
    mixed = column.astype(jnp.float32) + jnp.dot(
        mixing[0, 0], column, preferred_element_type=jnp.float32
    )
    out[0, 0, 0] = mixed.astype(jnp.bfloat16)
    row = lax.broadcasted_iota(jnp.int32, (16, column.shape[1]), 0)
    above = jnp.broadcast_to(top[pl.ds(field, 1), :], (16, column.shape[1]))
    out[0, 0, 0, 0:16, :] = jnp.where(row == 0, above, mixed[0:16, :]).astype(jnp.bfloat16)


def local(
    columns, mixing, lagged_flux, coefficients, ocean_mask, atm_tile, ocean_tile, live, weights
):
    _, _, fields, levels, cells = columns.shape
    width = weights.shape[3]
    tiles = cells // width
    count = lax.axis_size("blk")
    core, _, found = place()
    codes = atm_tile + 256 * ocean_tile + 65536 * live
    swap = swap_pairs(count)
    wide = exchange_pairs(count, 1)
    near = exchange_pairs(count, 0)
    field_f32 = jax.ShapeDtypeStruct((fields, cells), jnp.float32)
    field_bf16 = jax.ShapeDtypeStruct((fields, cells), jnp.bfloat16)

    level = pl.pallas_call(
        level_kernel,
        out_shape=field_f32,
        in_specs=[HBM, HBM, HBM],
        out_specs=VMEM,
        scratch_shapes=[
            pltpu.VMEM((fields, levels, cells), jnp.bfloat16),
            pltpu.VMEM((16, levels), jnp.bfloat16),
            pltpu.VMEM((fields, cells), jnp.bfloat16),
            pltpu.SemaphoreType.DMA((fields,)),
            pltpu.SemaphoreType.DMA((2,)),
        ],
        compiler_params=pltpu.CompilerParams(vmem_limit_bytes=24 << 20),
    )(*(pltpu.with_memory_space_constraint(x, pltpu.HBM) for x in (columns, mixing, lagged_flux)))
    level, weights = lax.optimization_barrier((level, weights))
    other_level = lax.ppermute(level, axes, swap)
    is_atm = core == 0
    surface = jnp.where(is_atm, level, other_level)
    ocean_level = jnp.where(is_atm, other_level, level)

    first, second, own = pl.pallas_call(
        remap_kernel,
        out_shape=(field_bf16, field_bf16, field_f32),
        in_specs=[SMEM, VMEM, VMEM],
        out_specs=(VMEM, VMEM, VMEM),
        scratch_shapes=[
            pltpu.VMEM((tiles, fields, width), jnp.float32),
            pltpu.VMEM((3, tiles, fields, width), jnp.float32),
        ],
        compiler_params=pltpu.CompilerParams(vmem_limit_bytes=24 << 20),
    )(codes, surface, weights)
    got_first = lax.ppermute(first, axes, wide)
    got_second = lax.ppermute(second, axes, near)
    partial = (
        own
        + jnp.where(found[0], got_first.astype(jnp.float32), 0.0)
        + jnp.where(found[1], got_second.astype(jnp.float32), 0.0)
    )
    remapped = partial + lax.ppermute(partial, axes, swap)

    difference = remapped - ocean_level
    speed = jnp.sqrt(
        difference[0:1] * difference[0:1] + difference[1:2] * difference[1:2] + 1.0
    )
    ocean_flux = (
        coefficients[:, None] * speed * difference * ocean_mask.astype(jnp.float32)
    ).astype(jnp.bfloat16)
    top = jnp.where(
        is_atm, surface, ocean_level + step_weight * ocean_flux.astype(jnp.float32)
    )

    flux_first = lax.ppermute(ocean_flux, axes, wide)
    flux_second = lax.ppermute(ocean_flux, axes, near)

    block = (1, 1, 1, levels, cells)
    new_columns, done = pl.pallas_call(
        mix_kernel,
        grid=(fields,),
        out_shape=(
            jax.ShapeDtypeStruct(columns.shape, jnp.bfloat16),
            jax.ShapeDtypeStruct((8, 128), jnp.float32),
        ),
        in_specs=[
            pl.BlockSpec(block, lambda f: (0, 0, f, 0, 0)),
            pl.BlockSpec((1, 1, levels, levels), lambda f: (0, 0, 0, 0)),
            pl.BlockSpec((fields, cells), lambda f: (0, 0)),
        ],
        out_specs=(
            pl.BlockSpec(block, lambda f: (0, 0, f, 0, 0)),
            pl.BlockSpec((8, 128), lambda f: (0, 0)),
        ),
        cost_estimate=pl.CostEstimate(
            flops=2 * fields * levels * levels * cells,
            transcendentals=0,
            bytes_accessed=4 * fields * levels * cells,
        ),
        compiler_params=pltpu.CompilerParams(vmem_limit_bytes=24 << 20),
    )(pltpu.with_memory_space_constraint(columns, pltpu.HBM), mixing, top)

    half = pl.pallas_call(
        back_kernel,
        out_shape=field_f32,
        in_specs=[SMEM, VMEM, VMEM, VMEM, VMEM, ANY],
        out_specs=VMEM,
        scratch_shapes=[
            pltpu.VMEM((3, tiles, fields, width), jnp.float32),
            pltpu.VMEM((2, tiles, fields, width), jnp.float32),
        ],
        compiler_params=pltpu.CompilerParams(vmem_limit_bytes=24 << 20),
    )(codes, flux_second, flux_first, ocean_flux, weights, done)
    atm_flux = (half + lax.ppermute(half, axes, swap)).astype(jnp.bfloat16)
    flux_here = jnp.where(is_atm, atm_flux, ocean_flux)
    return (new_columns, flux_here[None, None])


def solution(mesh):
    in_specs = (
        P("sec", "blk", None, None, None),
        P("sec", "blk", None, None),
        P("blk", None, None),
        P(),
        P("blk", None),
        P("blk", None, None),
        P("blk", None, None),
        P("blk", None, None),
        P("blk", None, None, None, None),
    )
    out_specs = (P("sec", "blk", None, None, None), P("sec", "blk", None, None))
    return jax.shard_map(local, mesh=mesh, in_specs=in_specs, out_specs=out_specs, check_vma=False)
```

```python
import jax
import jax.numpy as jnp
from jax import lax
from jax.experimental import pallas as pl
from jax.experimental.pallas import tpu as pltpu
from jax.sharding import PartitionSpec as P

step_weight = 0.25
axes = ("sec", "blk")
VMEM = pl.BlockSpec(memory_space=pltpu.VMEM)
SMEM = pl.BlockSpec(memory_space=pltpu.SMEM)
ANY = pl.BlockSpec(memory_space=pl.ANY)
HBM = pl.BlockSpec(memory_space=pltpu.HBM)


def partner(block, distance, phase, count):
    other = block + distance if (block // distance) % 2 == phase else block - distance
    return other if 0 <= other < count else block


def exchange_pairs(count, phase):
    first = [(b, partner(b, 2, phase, count)) for b in range(count)]
    second = [(count + b, count + partner(b, 1, phase, count)) for b in range(count)]
    return first + second


def swap_pairs(count):
    return [(b, count + b) for b in range(count)] + [(count + b, b) for b in range(count)]


def place():
    count = lax.axis_size("blk")
    core = lax.axis_index("sec")
    block = lax.axis_index("blk")
    reach = 2 - core
    shift = 1 - core
    place_in_pair = jnp.bitwise_and(lax.shift_right_logical(block, shift), 1)
    wide_step = jnp.where(place_in_pair == 1, reach, -reach)
    near_step = -wide_step
    found = []
    for step in (wide_step, near_step):
        other = block + step
        found.append(jnp.logical_and(other >= 0, other < count))
    return core, (wide_step + 2, near_step + 2), found


def level_kernel(columns, mixing, lagged, out, buffer, rows, late, semaphore, extra):
    fields = out.shape[0]
    small = [
        pltpu.make_async_copy(mixing.at[0, 0, 0:16], rows, extra.at[0]),
        pltpu.make_async_copy(lagged.at[0], late, extra.at[1]),
    ]
    copies = [
        pltpu.make_async_copy(columns.at[0, 0, f], buffer.at[f], semaphore.at[f])
        for f in range(fields)
    ]
    small[0].start()
    for copy in copies:
        copy.start()
    small[1].start()
    small[0].wait()
    for f in range(fields):
        if f % 4 == 0:
            for copy in copies[f : f + 4]:
                copy.wait()
        product = jnp.dot(rows[...], buffer[f], preferred_element_type=jnp.float32)
        level = product + buffer[f, 0:16, :].astype(jnp.float32)
        out[f : f + 1, :] = level[0:1, :]
    small[1].wait()

    @pl.when(lax.axis_index("sec") == 0)
    def _():
        surface = out[...] - step_weight * late[...].astype(jnp.float32)
        out[...] = surface.astype(jnp.bfloat16).astype(jnp.float32)


def pick_kernel(weights, after, picked, semaphore):
    del after
    core, distances, _ = place()
    slots = weights.shape[2]
    half = slots // 2
    copies = [
        pltpu.make_async_copy(
            weights.at[0, distances[g]], picked.at[pl.ds(g * slots, slots)], semaphore.at[g]
        )
        for g in (0, 1)
    ]
    copies.append(
        pltpu.make_async_copy(
            weights.at[0, 2, pl.ds(core * half, half)],
            picked.at[pl.ds(2 * slots, half)],
            semaphore.at[2],
        )
    )
    for copy in copies:
        copy.start()
    for copy in copies:
        copy.wait()


def slot_jobs(core, distances, slots):
    half = slots // 2
    jobs = [(g, distances[g], k, g * slots + k) for k in range(slots) for g in (0, 1)]
    return jobs + [(2, 2, k + core * half, 2 * slots + k) for k in range(half)]


def remap_kernel(codes, level, other, weights, first, second, own, ocean, tiles, sums):
    count, fields, width = tiles.shape
    core, distances, found = place()

    def spread(surface, below):
        for t in range(count):
            tiles[t] = surface[:, t * width : (t + 1) * width]
        ocean[...] = below[...]

    @pl.when(core == 0)
    def _():
        spread(level, other)

    @pl.when(core == 1)
    def _():
        spread(other, level)

    sums[...] = jnp.zeros_like(sums)
    for g, p, slot, at in slot_jobs(core, distances, codes.shape[2]):
        code = codes[0, p, slot]
        part = tiles[jnp.bitwise_and(code, 255)].astype(jnp.bfloat16)
        product = jnp.dot(part, weights[at], preferred_element_type=jnp.float32)
        product = product.astype(jnp.bfloat16).astype(jnp.float32)
        target = jnp.bitwise_and(lax.shift_right_logical(code, 8), 255)
        keep = lax.shift_right_logical(code, 16) == 1
        if g < 2:
            keep = jnp.logical_and(keep, found[g])
        sums[g, target] = sums[g, target] + jnp.where(keep, product, 0.0)
    for t in range(count):
        span = slice(t * width, (t + 1) * width)
        first[:, span] = sums[0, t].astype(jnp.bfloat16)
        second[:, span] = sums[1, t].astype(jnp.bfloat16)
        own[:, span] = sums[2, t]


def back_kernel(codes, second, first, own, weights, after, kept, sent, tiles, sums):
    del after
    _, count, fields, width = tiles.shape
    core, distances, found = place()
    for t in range(count):
        span = slice(t * width, (t + 1) * width)
        tiles[0, t] = first[:, span].astype(jnp.float32)
        tiles[1, t] = second[:, span].astype(jnp.float32)
        tiles[2, t] = own[:, span].astype(jnp.float32)
    sums[...] = jnp.zeros_like(sums)
    for i, (g, p, slot, at) in enumerate(slot_jobs(core, distances, codes.shape[2])):
        code = codes[0, p, slot]
        source = jnp.bitwise_and(lax.shift_right_logical(code, 8), 255)
        part = tiles[g, source].astype(jnp.bfloat16)
        product = lax.dot_general(
            part,
            weights[at],
            (((1,), (1,)), ((), ())),
            preferred_element_type=jnp.float32,
        )
        target = jnp.bitwise_and(code, 255)
        keep = lax.shift_right_logical(code, 16) == 1
        if g < 2:
            keep = jnp.logical_and(keep, found[g])
        sums[i % 2, target] = sums[i % 2, target] + jnp.where(keep, product, 0.0)

    @pl.when(core == 0)
    def _():
        for t in range(count):
            kept[:, t * width : (t + 1) * width] = sums[0, t] + sums[1, t]
        sent[...] = jnp.zeros_like(sent)

    @pl.when(core == 1)
    def _():
        for t in range(count):
            sent[:, t * width : (t + 1) * width] = sums[0, t] + sums[1, t]
        kept[...] = own[...].astype(jnp.float32)


def mix_kernel(held, mixing, level, flux, out, done, mixed, semaphore):
    share = jnp.where(lax.axis_index("sec") == 1, step_weight, 0.0)
    top = level[...] + share * flux[...].astype(jnp.float32)
    fields, levels, cells = held.shape
    row = lax.broadcasted_iota(jnp.int32, (16, cells), 0)
    copies = []
    for f in range(fields):
        total = held[f].astype(jnp.float32) + jnp.dot(
            mixing[0, 0], held[f], preferred_element_type=jnp.float32
        )
        mixed[f] = total.astype(jnp.bfloat16)
        above = jnp.broadcast_to(top[f : f + 1, :], (16, cells))
        mixed[f, 0:16, :] = jnp.where(row == 0, above, total[0:16, :]).astype(jnp.bfloat16)
        copies.append(pltpu.make_async_copy(mixed.at[f], out.at[0, 0, f], semaphore.at[f]))
        copies[f].start()
    done[...] = jnp.zeros_like(done)
    for copy in copies:
        copy.wait()


def local(
    columns, mixing, lagged_flux, coefficients, ocean_mask, atm_tile, ocean_tile, live, weights
):
    _, _, fields, levels, cells = columns.shape
    width = weights.shape[3]
    tiles = cells // width
    count = lax.axis_size("blk")
    codes = atm_tile + 256 * ocean_tile + 65536 * live
    swap = swap_pairs(count)
    wide = exchange_pairs(count, 1)
    near = exchange_pairs(count, 0)
    field_f32 = jax.ShapeDtypeStruct((fields, cells), jnp.float32)
    field_bf16 = jax.ShapeDtypeStruct((fields, cells), jnp.bfloat16)

    level, held = pl.pallas_call(
        level_kernel,
        out_shape=(field_f32, jax.ShapeDtypeStruct(columns.shape[2:], jnp.bfloat16)),
        in_specs=[HBM, HBM, HBM],
        out_specs=(VMEM, VMEM),
        scratch_shapes=[
            pltpu.VMEM((16, levels), jnp.bfloat16),
            pltpu.VMEM((fields, cells), jnp.bfloat16),
            pltpu.SemaphoreType.DMA((fields,)),
            pltpu.SemaphoreType.DMA((2,)),
        ],
        compiler_params=pltpu.CompilerParams(vmem_limit_bytes=8 << 20),
    )(*(pltpu.with_memory_space_constraint(x, pltpu.HBM) for x in (columns, mixing, lagged_flux)))
    slots = weights.shape[2]
    picked = pl.pallas_call(
        pick_kernel,
        out_shape=jax.ShapeDtypeStruct((5 * slots // 2, width, width), jnp.bfloat16),
        in_specs=[HBM, ANY],
        out_specs=VMEM,
        scratch_shapes=[pltpu.SemaphoreType.DMA((3,))],
        compiler_params=pltpu.CompilerParams(vmem_limit_bytes=8 << 20),
    )(pltpu.with_memory_space_constraint(weights, pltpu.HBM), level)
    other_level = lax.ppermute(level, axes, swap)
    first, second, own, ocean_level = pl.pallas_call(
        remap_kernel,
        out_shape=(field_bf16, field_bf16, field_f32, field_f32),
        in_specs=[SMEM, VMEM, VMEM, VMEM],
        out_specs=(VMEM, VMEM, VMEM, VMEM),
        scratch_shapes=[
            pltpu.VMEM((tiles, fields, width), jnp.float32),
            pltpu.VMEM((3, tiles, fields, width), jnp.float32),
        ],
        compiler_params=pltpu.CompilerParams(vmem_limit_bytes=8 << 20),
    )(codes, level, other_level, picked)
    got_first = lax.ppermute(first, axes, wide)
    got_second = lax.ppermute(second, axes, near)
    partial = own + got_first.astype(jnp.float32) + got_second.astype(jnp.float32)
    remapped = partial + lax.ppermute(partial, axes, swap)

    difference = remapped - ocean_level
    speed = jnp.sqrt(
        difference[0:1] * difference[0:1] + difference[1:2] * difference[1:2] + 1.0
    )
    ocean_flux = (
        coefficients[:, None] * speed * difference * ocean_mask.astype(jnp.float32)
    ).astype(jnp.bfloat16)
    flux_first = lax.ppermute(ocean_flux, axes, wide)
    flux_second = lax.ppermute(ocean_flux, axes, near)

    new_columns, done = pl.pallas_call(
        mix_kernel,
        out_shape=(
            jax.ShapeDtypeStruct(columns.shape, jnp.bfloat16),
            jax.ShapeDtypeStruct((8, 128), jnp.float32),
        ),
        in_specs=[VMEM, VMEM, VMEM, VMEM],
        out_specs=(ANY, VMEM),
        scratch_shapes=[
            pltpu.VMEM((fields, levels, cells), jnp.bfloat16),
            pltpu.SemaphoreType.DMA((fields,)),
        ],
        cost_estimate=pl.CostEstimate(
            flops=2 * fields * levels * levels * cells,
            transcendentals=0,
            bytes_accessed=4 * fields * levels * cells,
        ),
        compiler_params=pltpu.CompilerParams(vmem_limit_bytes=8 << 20),
    )(pltpu.with_memory_space_constraint(held, pltpu.VMEM), mixing, level, ocean_flux)

    kept, sent = pl.pallas_call(
        back_kernel,
        out_shape=(field_f32, field_f32),
        in_specs=[SMEM, VMEM, VMEM, VMEM, VMEM, ANY],
        out_specs=(VMEM, VMEM),
        scratch_shapes=[
            pltpu.VMEM((3, tiles, fields, width), jnp.float32),
            pltpu.VMEM((2, tiles, fields, width), jnp.float32),
        ],
        compiler_params=pltpu.CompilerParams(vmem_limit_bytes=8 << 20),
    )(codes, flux_second, flux_first, ocean_flux, picked, done)
    flux_here = (kept + lax.ppermute(sent, axes, swap)).astype(jnp.bfloat16)
    return (new_columns, flux_here[None, None])


def solution(mesh):
    in_specs = (
        P("sec", "blk", None, None, None),
        P("sec", "blk", None, None),
        P("blk", None, None),
        P(),
        P("blk", None),
        P("blk", None, None),
        P("blk", None, None),
        P("blk", None, None),
        P("blk", None, None, None, None),
    )
    out_specs = (P("sec", "blk", None, None, None), P("sec", "blk", None, None))
    return jax.shard_map(local, mesh=mesh, in_specs=in_specs, out_specs=out_specs, check_vma=False)
```

```python
import jax
import jax.numpy as jnp
from jax import lax
from jax.experimental import pallas as pl
from jax.experimental.pallas import tpu as pltpu
from jax.sharding import PartitionSpec as P

step_weight = 0.25
axes = ("sec", "blk")
VMEM = pl.BlockSpec(memory_space=pltpu.VMEM)
SMEM = pl.BlockSpec(memory_space=pltpu.SMEM)
ANY = pl.BlockSpec(memory_space=pl.ANY)
HBM = pl.BlockSpec(memory_space=pltpu.HBM)


def partner(block, distance, phase, count):
    other = block + distance if (block // distance) % 2 == phase else block - distance
    return other if 0 <= other < count else block


def exchange_pairs(count):
    lower, across, upper, alone = [], [], [], []
    for b in range(count):
        for core in (0, 1):
            me = core * count + b
            inside = (me, core * count + partner(b, 1 + core, 0, count))
            idle = (me, (1 - core) * count + b)
            lower.append(inside if b % 8 < 4 else idle)
            upper.append(idle if b % 8 < 4 else inside)
            other = partner(b, 2 - core, 1, count)
            if other == b:
                alone.append(me)
            else:
                across.append((me, core * count + other))
    low = [d for d in alone if d % count < count // 2]
    high = [d for d in alone if d % count >= count // 2]
    for ring in (low, high):
        across += [(d, ring[(i + 1) % len(ring)]) for i, d in enumerate(ring)]
    return lower, across, upper


def swap_pairs(count):
    return [(b, count + b) for b in range(count)] + [(count + b, b) for b in range(count)]


def place():
    count = lax.axis_size("blk")
    core = lax.axis_index("sec")
    block = lax.axis_index("blk")
    steps = []
    for distance, phase in ((2 - core, 1), (1 + core, 0)):
        position = jnp.bitwise_and(lax.shift_right_logical(block, distance - 1), 1)
        steps.append(jnp.where(position == phase, distance, -distance))
    found = []
    for step in steps:
        other = block + step
        found.append(jnp.logical_and(other >= 0, other < count))
    return core, (steps[0] + 2, steps[1] + 2), found


def in_lower_half():
    return jnp.bitwise_and(lax.axis_index("blk"), 7) < 4


def level_kernel(columns, mixing, lagged, out, buffer, rows, late, semaphore, extra):
    fields = out.shape[0]
    small = [
        pltpu.make_async_copy(mixing.at[0, 0, 0:16], rows, extra.at[0]),
        pltpu.make_async_copy(lagged.at[0], late, extra.at[1]),
    ]
    copies = [
        pltpu.make_async_copy(columns.at[0, 0, f], buffer.at[f], semaphore.at[f])
        for f in range(fields)
    ]
    small[0].start()
    for copy in copies:
        copy.start()
    small[1].start()
    small[0].wait()
    for f in range(fields):
        if f % 4 == 0:
            for copy in copies[f : f + 4]:
                copy.wait()
        product = jnp.dot(rows[...], buffer[f], preferred_element_type=jnp.float32)
        level = product + buffer[f, 0:16, :].astype(jnp.float32)
        out[f : f + 1, :] = level[0:1, :]
    small[1].wait()

    @pl.when(lax.axis_index("sec") == 0)
    def _():
        surface = out[...] - step_weight * late[...].astype(jnp.float32)
        out[...] = surface.astype(jnp.bfloat16).astype(jnp.float32)


def pick_kernel(weights, after, picked, semaphore):
    del after
    core, distances, _ = place()
    slots = weights.shape[2]
    half = slots // 2
    copies = [
        pltpu.make_async_copy(
            weights.at[0, distances[g]], picked.at[pl.ds(g * slots, slots)], semaphore.at[g]
        )
        for g in (0, 1)
    ]
    copies.append(
        pltpu.make_async_copy(
            weights.at[0, 2, pl.ds(core * half, half)],
            picked.at[pl.ds(2 * slots, half)],
            semaphore.at[2],
        )
    )
    for copy in copies:
        copy.start()
    for copy in copies:
        copy.wait()


def slot_jobs(core, distances, slots):
    half = slots // 2
    jobs = [(g, distances[g], k, g * slots + k) for k in range(slots) for g in (0, 1)]
    return jobs + [(2, 2, k + core * half, 2 * slots + k) for k in range(half)]


def remap_kernel(codes, level, other, weights, across, inside, own, ocean, tiles, sums):
    count, fields, width = tiles.shape
    core, distances, found = place()

    def spread(surface, below):
        for t in range(count):
            tiles[t] = surface[:, t * width : (t + 1) * width]
        ocean[...] = below[...]

    @pl.when(core == 0)
    def _():
        spread(level, other)

    @pl.when(core == 1)
    def _():
        spread(other, level)

    sums[...] = jnp.zeros_like(sums)
    for g, p, slot, at in slot_jobs(core, distances, codes.shape[2]):
        code = codes[0, p, slot]
        part = tiles[jnp.bitwise_and(code, 255)].astype(jnp.bfloat16)
        product = jnp.dot(part, weights[at], preferred_element_type=jnp.float32)
        product = product.astype(jnp.bfloat16).astype(jnp.float32)
        target = jnp.bitwise_and(lax.shift_right_logical(code, 8), 255)
        keep = lax.shift_right_logical(code, 16) == 1
        if g < 2:
            keep = jnp.logical_and(keep, found[g])
        sums[g, target] = sums[g, target] + jnp.where(keep, product, 0.0)
    for t in range(count):
        span = slice(t * width, (t + 1) * width)
        across[:, span] = sums[0, t].astype(jnp.bfloat16)
        inside[:, span] = sums[1, t].astype(jnp.bfloat16)
        own[:, span] = sums[2, t]


def back_kernel(codes, across, inside, own, weights, after, kept, sent, tiles, sums):
    del after
    _, count, fields, width = tiles.shape
    core, distances, found = place()
    for t in range(count):
        span = slice(t * width, (t + 1) * width)
        tiles[0, t] = across[:, span].astype(jnp.float32)
        tiles[1, t] = inside[:, span].astype(jnp.float32)
        tiles[2, t] = own[:, span].astype(jnp.float32)
    sums[...] = jnp.zeros_like(sums)
    for i, (g, p, slot, at) in enumerate(slot_jobs(core, distances, codes.shape[2])):
        code = codes[0, p, slot]
        source = jnp.bitwise_and(lax.shift_right_logical(code, 8), 255)
        part = tiles[g, source].astype(jnp.bfloat16)
        product = lax.dot_general(
            part,
            weights[at],
            (((1,), (1,)), ((), ())),
            preferred_element_type=jnp.float32,
        )
        target = jnp.bitwise_and(code, 255)
        keep = lax.shift_right_logical(code, 16) == 1
        if g < 2:
            keep = jnp.logical_and(keep, found[g])
        sums[i % 2, target] = sums[i % 2, target] + jnp.where(keep, product, 0.0)

    @pl.when(core == 0)
    def _():
        for t in range(count):
            kept[:, t * width : (t + 1) * width] = sums[0, t] + sums[1, t]
        sent[...] = jnp.zeros_like(sent)

    @pl.when(core == 1)
    def _():
        for t in range(count):
            sent[:, t * width : (t + 1) * width] = sums[0, t] + sums[1, t]
        kept[...] = own[...].astype(jnp.float32)


def mix_kernel(held, mixing, own, out, head, passed, mixed, semaphore):
    fields, levels, _ = held.shape
    rows = head.shape[1]
    copies = []
    for f in range(fields):
        total = held[f].astype(jnp.float32) + jnp.dot(
            mixing[0, 0], held[f], preferred_element_type=jnp.float32
        )
        head[f] = total[0:rows].astype(jnp.bfloat16)
        mixed[f] = total[rows:].astype(jnp.bfloat16)
        copies.append(
            pltpu.make_async_copy(
                mixed.at[f], out.at[0, 0, f, pl.ds(rows, levels - rows)], semaphore.at[f]
            )
        )
        copies[f].start()
    passed[...] = own[...]
    for copy in copies:
        copy.wait()


def top_kernel(head, level, flux, columns, out, done, tops, semaphore):
    del columns
    fields, rows, cells = head.shape
    share = jnp.where(lax.axis_index("sec") == 1, step_weight, 0.0)
    top = level[...] + share * flux[...].astype(jnp.float32)
    row = lax.broadcasted_iota(jnp.int32, (rows, cells), 0)
    copies = []
    for f in range(fields):
        above = jnp.broadcast_to(top[f : f + 1, :], (rows, cells))
        tops[f] = jnp.where(row == 0, above, head[f].astype(jnp.float32)).astype(jnp.bfloat16)
        copies.append(
            pltpu.make_async_copy(tops.at[f], out.at[0, 0, f, pl.ds(0, rows)], semaphore.at[f])
        )
        copies[f].start()
    done[...] = jnp.zeros_like(done)
    for copy in copies:
        copy.wait()


def local(
    columns, mixing, lagged_flux, coefficients, ocean_mask, atm_tile, ocean_tile, live, weights
):
    _, _, fields, levels, cells = columns.shape
    width = weights.shape[3]
    tiles = cells // width
    count = lax.axis_size("blk")
    codes = atm_tile + 256 * ocean_tile + 65536 * live
    swap = swap_pairs(count)
    lower, across, upper = exchange_pairs(count)
    inside = [a if a[0] % count % 8 < 4 else b for a, b in zip(lower, upper)]
    field_f32 = jax.ShapeDtypeStruct((fields, cells), jnp.float32)
    field_bf16 = jax.ShapeDtypeStruct((fields, cells), jnp.bfloat16)

    level, held = pl.pallas_call(
        level_kernel,
        out_shape=(field_f32, jax.ShapeDtypeStruct(columns.shape[2:], jnp.bfloat16)),
        in_specs=[HBM, HBM, HBM],
        out_specs=(VMEM, VMEM),
        scratch_shapes=[
            pltpu.VMEM((16, levels), jnp.bfloat16),
            pltpu.VMEM((fields, cells), jnp.bfloat16),
            pltpu.SemaphoreType.DMA((fields,)),
            pltpu.SemaphoreType.DMA((2,)),
        ],
        compiler_params=pltpu.CompilerParams(vmem_limit_bytes=8 << 20),
    )(*(pltpu.with_memory_space_constraint(x, pltpu.HBM) for x in (columns, mixing, lagged_flux)))
    slots = weights.shape[2]
    picked = pl.pallas_call(
        pick_kernel,
        out_shape=jax.ShapeDtypeStruct((5 * slots // 2, width, width), jnp.bfloat16),
        in_specs=[HBM, ANY],
        out_specs=VMEM,
        scratch_shapes=[pltpu.SemaphoreType.DMA((3,))],
        compiler_params=pltpu.CompilerParams(vmem_limit_bytes=8 << 20),
    )(pltpu.with_memory_space_constraint(weights, pltpu.HBM), level)
    other_level = lax.ppermute(level, axes, swap)
    to_across, to_inside, own, ocean_level = pl.pallas_call(
        remap_kernel,
        out_shape=(field_bf16, field_bf16, field_f32, field_f32),
        in_specs=[SMEM, VMEM, VMEM, VMEM],
        out_specs=(VMEM,) * 4,
        scratch_shapes=[
            pltpu.VMEM((tiles, fields, width), jnp.float32),
            pltpu.VMEM((3, tiles, fields, width), jnp.float32),
        ],
        compiler_params=pltpu.CompilerParams(vmem_limit_bytes=8 << 20),
    )(codes, level, other_level, picked)
    most_columns, head, own = pl.pallas_call(
        mix_kernel,
        out_shape=(
            jax.ShapeDtypeStruct(columns.shape, jnp.bfloat16),
            jax.ShapeDtypeStruct((fields, 16, cells), jnp.bfloat16),
            field_f32,
        ),
        in_specs=[VMEM, VMEM, VMEM],
        out_specs=(HBM, VMEM, VMEM),
        scratch_shapes=[
            pltpu.VMEM((fields, levels - 16, cells), jnp.bfloat16),
            pltpu.SemaphoreType.DMA((fields,)),
        ],
        cost_estimate=pl.CostEstimate(
            flops=2 * fields * levels * levels * cells,
            transcendentals=0,
            bytes_accessed=4 * fields * levels * cells,
        ),
        compiler_params=pltpu.CompilerParams(vmem_limit_bytes=16 << 20),
    )(pltpu.with_memory_space_constraint(held, pltpu.VMEM), mixing, own)
    partial = own
    for part, pairs in ((to_across, across), (to_inside, inside)):
        partial = partial + lax.ppermute(part, axes, pairs).astype(jnp.float32)
    remapped = partial + lax.ppermute(partial, axes, swap)

    difference = remapped - ocean_level
    speed = jnp.sqrt(
        difference[0:1] * difference[0:1] + difference[1:2] * difference[1:2] + 1.0
    )
    ocean_flux = (
        coefficients[:, None] * speed * difference * ocean_mask.astype(jnp.float32)
    ).astype(jnp.bfloat16)
    flux_across = lax.ppermute(ocean_flux, axes, across)
    flux_inside = lax.ppermute(ocean_flux, axes, inside)

    new_columns, done = pl.pallas_call(
        top_kernel,
        out_shape=(
            jax.ShapeDtypeStruct(columns.shape, jnp.bfloat16),
            jax.ShapeDtypeStruct((8, 128), jnp.float32),
        ),
        in_specs=[VMEM, VMEM, VMEM, HBM],
        out_specs=(HBM, VMEM),
        input_output_aliases={3: 0},
        scratch_shapes=[
            pltpu.VMEM((fields, 16, cells), jnp.bfloat16),
            pltpu.SemaphoreType.DMA((fields,)),
        ],
        compiler_params=pltpu.CompilerParams(vmem_limit_bytes=8 << 20),
    )(head, level, ocean_flux, most_columns)

    kept, sent = pl.pallas_call(
        back_kernel,
        out_shape=(field_f32, field_f32),
        in_specs=[SMEM, VMEM, VMEM, VMEM, VMEM, ANY],
        out_specs=(VMEM, VMEM),
        scratch_shapes=[
            pltpu.VMEM((3, tiles, fields, width), jnp.float32),
            pltpu.VMEM((2, tiles, fields, width), jnp.float32),
        ],
        compiler_params=pltpu.CompilerParams(vmem_limit_bytes=8 << 20),
    )(codes, flux_across, flux_inside, ocean_flux, picked, done)
    flux_here = (kept + lax.ppermute(sent, axes, swap)).astype(jnp.bfloat16)
    return (new_columns, flux_here[None, None])


def solution(mesh):
    in_specs = (
        P("sec", "blk", None, None, None),
        P("sec", "blk", None, None),
        P("blk", None, None),
        P(),
        P("blk", None),
        P("blk", None, None),
        P("blk", None, None),
        P("blk", None, None),
        P("blk", None, None, None, None),
    )
    out_specs = (P("sec", "blk", None, None, None), P("sec", "blk", None, None))
    return jax.shard_map(local, mesh=mesh, in_specs=in_specs, out_specs=out_specs, check_vma=False)
```

```python
import jax
import jax.numpy as jnp
from jax import lax
from jax.experimental import pallas as pl
from jax.experimental.pallas import tpu as pltpu
from jax.sharding import PartitionSpec as P

step_weight = 0.25
axes = ("sec", "blk")
VMEM = pl.BlockSpec(memory_space=pltpu.VMEM)
ANY = pl.BlockSpec(memory_space=pl.ANY)
HBM = pl.BlockSpec(memory_space=pltpu.HBM)


def partner(block, distance, phase, count):
    other = block + distance if (block // distance) % 2 == phase else block - distance
    return other if 0 <= other < count else block


def exchange_pairs(count):
    lower, across, upper, alone = [], [], [], []
    for b in range(count):
        for core in (0, 1):
            me = core * count + b
            inside = (me, core * count + partner(b, 1 + core, 0, count))
            idle = (me, (1 - core) * count + b)
            lower.append(inside if b % 8 < 4 else idle)
            upper.append(idle if b % 8 < 4 else inside)
            other = partner(b, 2 - core, 1, count)
            if other == b:
                alone.append(me)
            else:
                across.append((me, core * count + other))
    low = [d for d in alone if d % count < count // 2]
    high = [d for d in alone if d % count >= count // 2]
    for ring in (low, high):
        across += [(d, ring[(i + 1) % len(ring)]) for i, d in enumerate(ring)]
    return lower, across, upper


def swap_pairs(count):
    return [(b, count + b) for b in range(count)] + [(count + b, b) for b in range(count)]


def place():
    count = lax.axis_size("blk")
    core = lax.axis_index("sec")
    block = lax.axis_index("blk")
    steps = []
    for distance, phase in ((2 - core, 1), (1 + core, 0)):
        position = jnp.bitwise_and(lax.shift_right_logical(block, distance - 1), 1)
        steps.append(jnp.where(position == phase, distance, -distance))
    found = []
    for step in steps:
        other = block + step
        found.append(jnp.logical_and(other >= 0, other < count))
    return core, (steps[0] + 2, steps[1] + 2), found


def level_kernel(
    columns, mixing, lagged, weights, out, buffer, picked, rows, late, semaphore, extra, others
):
    fields = out.shape[0]
    small = [
        pltpu.make_async_copy(mixing.at[0, 0, 0:16], rows, extra.at[0]),
        pltpu.make_async_copy(lagged.at[0], late, extra.at[1]),
    ]
    copies = [
        pltpu.make_async_copy(columns.at[0, 0, f], buffer.at[f], semaphore.at[f])
        for f in range(fields)
    ]
    small[0].start()
    for copy in copies:
        copy.start()
    small[1].start()
    picks = pick_copies(weights, picked, others)
    for copy in picks:
        copy.start()
    small[0].wait()
    for f in range(fields):
        if f % 4 == 0:
            for copy in copies[f : f + 4]:
                copy.wait()
        product = jnp.dot(rows[...], buffer[f], preferred_element_type=jnp.float32)
        level = product + buffer[f, 0:16, :].astype(jnp.float32)
        out[f : f + 1, :] = level[0:1, :]
    small[1].wait()

    @pl.when(lax.axis_index("sec") == 0)
    def _():
        surface = out[...] - step_weight * late[...].astype(jnp.float32)
        out[...] = surface.astype(jnp.bfloat16).astype(jnp.float32)

    for copy in picks:
        copy.wait()


def pick_copies(weights, picked, semaphore):
    core, distances, _ = place()
    slots = weights.shape[2]
    half = slots // 2
    copies = [
        pltpu.make_async_copy(
            weights.at[0, distances[g]], picked.at[pl.ds(g * slots, slots)], semaphore.at[g]
        )
        for g in (0, 1)
    ]
    copies.append(
        pltpu.make_async_copy(
            weights.at[0, 2, pl.ds(core * half, half)],
            picked.at[pl.ds(2 * slots, half)],
            semaphore.at[2],
        )
    )
    return copies


def slot_jobs(core, distances, slots):
    half = slots // 2
    jobs = [(g, distances[g], k, g * slots + k) for k in range(slots) for g in (0, 1)]
    return jobs + [(2, 2, k + core * half, 2 * slots + k) for k in range(half)]


def remap(slots, surface, weights, across, inside, own, codes, semaphore, tiles, sums):
    count, fields, width = tiles.shape
    core, distances, found = place()
    fetch = pltpu.make_async_copy(slots, codes, semaphore)
    fetch.start()
    for t in range(count):
        tiles[t] = surface[:, t * width : (t + 1) * width]
    sums[...] = jnp.zeros_like(sums)
    fetch.wait()
    for g, p, slot, at in slot_jobs(core, distances, codes.shape[2]):
        code = codes[0, p, slot]
        part = tiles[jnp.bitwise_and(code, 255)].astype(jnp.bfloat16)
        product = jnp.dot(part, weights[at], preferred_element_type=jnp.float32)
        product = product.astype(jnp.bfloat16).astype(jnp.float32)
        target = jnp.bitwise_and(lax.shift_right_logical(code, 8), 255)
        keep = lax.shift_right_logical(code, 16) == 1
        if g < 2:
            keep = jnp.logical_and(keep, found[g])
        sums[g, target] = sums[g, target] + jnp.where(keep, product, 0.0)
    for t in range(count):
        span = slice(t * width, (t + 1) * width)
        across[:, span] = sums[0, t].astype(jnp.bfloat16)
        inside[:, span] = sums[1, t].astype(jnp.bfloat16)
        own[:, span] = sums[2, t]


def first_remap_kernel(slots, level, weights, across, inside, own, *scratch):
    @pl.when(lax.axis_index("sec") == 0)
    def _():
        remap(slots, level, weights, across, inside, own, *scratch)


def second_remap_kernel(
    slots, level, other, weights, across_0, inside_0, own_0, across, inside, own, ocean, *scratch
):
    core = lax.axis_index("sec")

    @pl.when(core == 0)
    def _():
        across[...] = across_0[...]
        inside[...] = inside_0[...]
        own[...] = own_0[...]
        ocean[...] = other[...]

    @pl.when(core == 1)
    def _():
        remap(slots, other, weights, across, inside, own, *scratch)
        ocean[...] = level[...]


def back_kernel(
    slots, across, inside, own, weights, after, kept, sent, codes, semaphore, tiles, sums
):
    del after
    fetch = pltpu.make_async_copy(slots, codes, semaphore)
    fetch.start()
    _, count, fields, width = tiles.shape
    core, distances, found = place()
    for t in range(count):
        span = slice(t * width, (t + 1) * width)
        tiles[0, t] = across[:, span].astype(jnp.float32)
        tiles[1, t] = inside[:, span].astype(jnp.float32)
        tiles[2, t] = own[:, span].astype(jnp.float32)
    sums[...] = jnp.zeros_like(sums)
    fetch.wait()
    for i, (g, p, slot, at) in enumerate(slot_jobs(core, distances, codes.shape[2])):
        code = codes[0, p, slot]
        source = jnp.bitwise_and(lax.shift_right_logical(code, 8), 255)
        part = tiles[g, source].astype(jnp.bfloat16)
        product = lax.dot_general(
            part,
            weights[at],
            (((1,), (1,)), ((), ())),
            preferred_element_type=jnp.float32,
        )
        target = jnp.bitwise_and(code, 255)
        keep = lax.shift_right_logical(code, 16) == 1
        if g < 2:
            keep = jnp.logical_and(keep, found[g])
        sums[i % 2, target] = sums[i % 2, target] + jnp.where(keep, product, 0.0)

    @pl.when(core == 0)
    def _():
        for t in range(count):
            kept[:, t * width : (t + 1) * width] = sums[0, t] + sums[1, t]
        sent[...] = jnp.zeros_like(sent)

    @pl.when(core == 1)
    def _():
        for t in range(count):
            sent[:, t * width : (t + 1) * width] = sums[0, t] + sums[1, t]
        kept[...] = own[...].astype(jnp.float32)


def mix_kernel(held, mixing, own, out, head, passed, mixed, semaphore):
    fields, levels, _ = held.shape
    rows = head.shape[1]
    copies = []
    for f in range(fields):
        total = held[f].astype(jnp.float32) + jnp.dot(
            mixing[0, 0], held[f], preferred_element_type=jnp.float32
        )
        head[f] = total[0:rows].astype(jnp.bfloat16)
        mixed[f] = total[rows:].astype(jnp.bfloat16)
        copies.append(
            pltpu.make_async_copy(
                mixed.at[f], out.at[0, 0, f, pl.ds(rows, levels - rows)], semaphore.at[f]
            )
        )
        copies[f].start()
    passed[...] = own[...]
    for copy in copies:
        copy.wait()


def top_kernel(head, level, flux, columns, out, done, tops, semaphore):
    del columns
    fields, rows, cells = head.shape
    share = jnp.where(lax.axis_index("sec") == 1, step_weight, 0.0)
    top = level[...] + share * flux[...].astype(jnp.float32)
    row = lax.broadcasted_iota(jnp.int32, (rows, cells), 0)
    copies = []
    for f in range(fields):
        above = jnp.broadcast_to(top[f : f + 1, :], (rows, cells))
        tops[f] = jnp.where(row == 0, above, head[f].astype(jnp.float32)).astype(jnp.bfloat16)
        copies.append(
            pltpu.make_async_copy(tops.at[f], out.at[0, 0, f, pl.ds(0, rows)], semaphore.at[f])
        )
        copies[f].start()
    done[...] = jnp.zeros_like(done)
    for copy in copies:
        copy.wait()


def local(
    columns, mixing, lagged_flux, coefficients, ocean_mask, atm_tile, ocean_tile, live, weights
):
    _, _, fields, levels, cells = columns.shape
    width = weights.shape[3]
    tiles = cells // width
    count = lax.axis_size("blk")
    codes = atm_tile + 256 * ocean_tile + 65536 * live
    swap = swap_pairs(count)
    lower, across, upper = exchange_pairs(count)
    inside = [a if a[0] % count % 8 < 4 else b for a, b in zip(lower, upper)]
    field_f32 = jax.ShapeDtypeStruct((fields, cells), jnp.float32)
    field_bf16 = jax.ShapeDtypeStruct((fields, cells), jnp.bfloat16)

    slots = weights.shape[2]
    level, held, picked = pl.pallas_call(
        level_kernel,
        out_shape=(
            field_f32,
            jax.ShapeDtypeStruct(columns.shape[2:], jnp.bfloat16),
            jax.ShapeDtypeStruct((5 * slots // 2, width, width), jnp.bfloat16),
        ),
        in_specs=[HBM, HBM, HBM, HBM],
        out_specs=(VMEM, VMEM, VMEM),
        scratch_shapes=[
            pltpu.VMEM((16, levels), jnp.bfloat16),
            pltpu.VMEM((fields, cells), jnp.bfloat16),
            pltpu.SemaphoreType.DMA((fields,)),
            pltpu.SemaphoreType.DMA((2,)),
            pltpu.SemaphoreType.DMA((3,)),
        ],
        compiler_params=pltpu.CompilerParams(vmem_limit_bytes=8 << 20),
    )(*(pltpu.with_memory_space_constraint(x, pltpu.HBM) for x in (columns, mixing, lagged_flux, weights)))
    other_level = lax.ppermute(level, axes, swap)

    scratch = [
        pltpu.SMEM(codes.shape, jnp.int32),
        pltpu.SemaphoreType.DMA,
        pltpu.VMEM((tiles, fields, width), jnp.float32),
        pltpu.VMEM((3, tiles, fields, width), jnp.float32),
    ]
    early = pl.pallas_call(
        first_remap_kernel,
        out_shape=(field_bf16, field_bf16, field_f32),
        in_specs=[VMEM, VMEM, VMEM],
        out_specs=(VMEM,) * 3,
        scratch_shapes=scratch,
        cost_estimate=pl.CostEstimate(
            flops=5 * slots * fields * width * width,
            transcendentals=0,
            bytes_accessed=5 * slots * width * width,
        ),
        compiler_params=pltpu.CompilerParams(vmem_limit_bytes=8 << 20),
    )(codes, level, picked)
    to_across, to_inside, own, ocean_level = pl.pallas_call(
        second_remap_kernel,
        out_shape=(field_bf16, field_bf16, field_f32, field_f32),
        in_specs=[VMEM] * 7,
        out_specs=(VMEM,) * 4,
        scratch_shapes=scratch,
        compiler_params=pltpu.CompilerParams(vmem_limit_bytes=8 << 20),
    )(codes, level, other_level, picked, *early)
    most_columns, head, own = pl.pallas_call(
        mix_kernel,
        out_shape=(
            jax.ShapeDtypeStruct(columns.shape, jnp.bfloat16),
            jax.ShapeDtypeStruct((fields, 16, cells), jnp.bfloat16),
            field_f32,
        ),
        in_specs=[VMEM, VMEM, VMEM],
        out_specs=(HBM, VMEM, VMEM),
        scratch_shapes=[
            pltpu.VMEM((fields, levels - 16, cells), jnp.bfloat16),
            pltpu.SemaphoreType.DMA((fields,)),
        ],
        cost_estimate=pl.CostEstimate(
            flops=2 * fields * levels * levels * cells,
            transcendentals=0,
            bytes_accessed=4 * fields * levels * cells,
        ),
        compiler_params=pltpu.CompilerParams(vmem_limit_bytes=16 << 20),
    )(pltpu.with_memory_space_constraint(held, pltpu.VMEM), mixing, own)
    partial = own
    for part, pairs in ((to_across, across), (to_inside, inside)):
        partial = partial + lax.ppermute(part, axes, pairs).astype(jnp.float32)
    remapped = partial + lax.ppermute(partial, axes, swap)

    difference = remapped - ocean_level
    speed = jnp.sqrt(
        difference[0:1] * difference[0:1] + difference[1:2] * difference[1:2] + 1.0
    )
    ocean_flux = (
        coefficients[:, None] * speed * difference * ocean_mask.astype(jnp.float32)
    ).astype(jnp.bfloat16)
    flux_across = lax.ppermute(ocean_flux, axes, across)
    flux_inside = lax.ppermute(ocean_flux, axes, inside)

    new_columns, done = pl.pallas_call(
        top_kernel,
        out_shape=(
            jax.ShapeDtypeStruct(columns.shape, jnp.bfloat16),
            jax.ShapeDtypeStruct((8, 128), jnp.float32),
        ),
        in_specs=[VMEM, VMEM, VMEM, HBM],
        out_specs=(HBM, VMEM),
        input_output_aliases={3: 0},
        scratch_shapes=[
            pltpu.VMEM((fields, 16, cells), jnp.bfloat16),
            pltpu.SemaphoreType.DMA((fields,)),
        ],
        compiler_params=pltpu.CompilerParams(vmem_limit_bytes=8 << 20),
    )(head, level, ocean_flux, most_columns)

    kept, sent = pl.pallas_call(
        back_kernel,
        out_shape=(field_f32, field_f32),
        in_specs=[VMEM, VMEM, VMEM, VMEM, VMEM, ANY],
        out_specs=(VMEM, VMEM),
        scratch_shapes=[
            pltpu.SMEM(codes.shape, jnp.int32),
            pltpu.SemaphoreType.DMA,
            pltpu.VMEM((3, tiles, fields, width), jnp.float32),
            pltpu.VMEM((2, tiles, fields, width), jnp.float32),
        ],
        compiler_params=pltpu.CompilerParams(vmem_limit_bytes=8 << 20),
    )(codes, flux_across, flux_inside, ocean_flux, picked, done)
    flux_here = (kept + lax.ppermute(sent, axes, swap)).astype(jnp.bfloat16)
    return (new_columns, flux_here[None, None])


def solution(mesh):
    in_specs = (
        P("sec", "blk", None, None, None),
        P("sec", "blk", None, None),
        P("blk", None, None),
        P(),
        P("blk", None),
        P("blk", None, None),
        P("blk", None, None),
        P("blk", None, None),
        P("blk", None, None, None, None),
    )
    out_specs = (P("sec", "blk", None, None, None), P("sec", "blk", None, None))
    return jax.shard_map(local, mesh=mesh, in_specs=in_specs, out_specs=out_specs, check_vma=False)
```

```python
import jax
import jax.numpy as jnp
from jax import lax
from jax.experimental import pallas as pl
from jax.experimental.pallas import tpu as pltpu
from jax.sharding import PartitionSpec as P

step_weight = 0.25
axes = ("sec", "blk")
VMEM = pl.BlockSpec(memory_space=pltpu.VMEM)
ANY = pl.BlockSpec(memory_space=pl.ANY)
HBM = pl.BlockSpec(memory_space=pltpu.HBM)


def partner(block, distance, phase, count):
    other = block + distance if (block // distance) % 2 == phase else block - distance
    return other if 0 <= other < count else block


def exchange_pairs(count):
    lower, across, upper, alone = [], [], [], []
    for b in range(count):
        for core in (0, 1):
            me = core * count + b
            inside = (me, core * count + partner(b, 1 + core, 0, count))
            idle = (me, (1 - core) * count + b)
            lower.append(inside if b % 8 < 4 else idle)
            upper.append(idle if b % 8 < 4 else inside)
            other = partner(b, 2 - core, 1, count)
            if other == b:
                alone.append(me)
            else:
                across.append((me, core * count + other))
    low = [d for d in alone if d % count < count // 2]
    high = [d for d in alone if d % count >= count // 2]
    for ring in (low, high):
        across += [(d, ring[(i + 1) % len(ring)]) for i, d in enumerate(ring)]
    return lower, across, upper


def swap_pairs(count):
    return [(b, count + b) for b in range(count)] + [(count + b, b) for b in range(count)]


def place():
    count = lax.axis_size("blk")
    core = lax.axis_index("sec")
    block = lax.axis_index("blk")
    steps = []
    for distance, phase in ((2 - core, 1), (1 + core, 0)):
        position = jnp.bitwise_and(lax.shift_right_logical(block, distance - 1), 1)
        steps.append(jnp.where(position == phase, distance, -distance))
    found = []
    for step in steps:
        other = block + step
        found.append(jnp.logical_and(other >= 0, other < count))
    return core, (steps[0] + 2, steps[1] + 2), found


def level_kernel(
    columns, mixing, lagged, weights, out, buffer, picked, rows, late, semaphore, extra, others
):
    fields = out.shape[0]
    small = [
        pltpu.make_async_copy(mixing.at[0, 0, 0:16], rows, extra.at[0]),
        pltpu.make_async_copy(lagged.at[0], late, extra.at[1]),
    ]
    copies = [
        pltpu.make_async_copy(columns.at[0, 0, f], buffer.at[f], semaphore.at[f])
        for f in range(fields)
    ]
    small[0].start()
    for copy in copies:
        copy.start()
    small[1].start()
    picks = pick_copies(weights, picked, others)
    for copy in picks:
        copy.start()
    small[0].wait()
    for f in range(fields):
        if f % 4 == 0:
            for copy in copies[f : f + 4]:
                copy.wait()
        product = jnp.dot(rows[...], buffer[f], preferred_element_type=jnp.float32)
        level = product + buffer[f, 0:16, :].astype(jnp.float32)
        out[f : f + 1, :] = level[0:1, :]
    small[1].wait()

    @pl.when(lax.axis_index("sec") == 0)
    def _():
        surface = out[...] - step_weight * late[...].astype(jnp.float32)
        out[...] = surface.astype(jnp.bfloat16).astype(jnp.float32)

    for copy in picks:
        copy.wait()


def pick_copies(weights, picked, semaphore):
    core, distances, _ = place()
    slots = weights.shape[2]
    half = slots // 2
    copies = [
        pltpu.make_async_copy(
            weights.at[0, distances[g]], picked.at[pl.ds(g * slots, slots)], semaphore.at[g]
        )
        for g in (0, 1)
    ]
    copies.append(
        pltpu.make_async_copy(
            weights.at[0, 2, pl.ds(core * half, half)],
            picked.at[pl.ds(2 * slots, half)],
            semaphore.at[2],
        )
    )
    return copies


def slot_jobs(core, distances, slots):
    half = slots // 2
    jobs = [(g, distances[g], k, g * slots + k) for k in range(slots) for g in (0, 1)]
    return jobs + [(2, 2, k + core * half, 2 * slots + k) for k in range(half)]


def remap(slots, surface, weights, across, inside, own, codes, semaphore, tiles, sums):
    count, fields, width = tiles.shape
    core, distances, found = place()
    fetch = pltpu.make_async_copy(slots, codes, semaphore)
    fetch.start()
    for t in range(count):
        tiles[t] = surface[:, t * width : (t + 1) * width]
    sums[...] = jnp.zeros_like(sums)
    fetch.wait()
    for g, p, slot, at in slot_jobs(core, distances, codes.shape[2]):
        code = codes[0, p, slot]
        part = tiles[jnp.bitwise_and(code, 255)].astype(jnp.bfloat16)
        product = jnp.dot(part, weights[at], preferred_element_type=jnp.float32)
        product = product.astype(jnp.bfloat16).astype(jnp.float32)
        target = jnp.bitwise_and(lax.shift_right_logical(code, 8), 255)
        keep = lax.shift_right_logical(code, 16) == 1
        if g < 2:
            keep = jnp.logical_and(keep, found[g])
        sums[g, target] = sums[g, target] + jnp.where(keep, product, 0.0)
    for t in range(count):
        span = slice(t * width, (t + 1) * width)
        across[:, span] = sums[0, t].astype(jnp.bfloat16)
        inside[:, span] = sums[1, t].astype(jnp.bfloat16)
        own[:, span] = sums[2, t]


def first_remap_kernel(slots, level, weights, across, inside, own, *scratch):
    @pl.when(lax.axis_index("sec") == 0)
    def _():
        remap(slots, level, weights, across, inside, own, *scratch)


def second_remap_kernel(
    slots, level, other, weights, across_0, inside_0, own_0, across, inside, own, ocean, *scratch
):
    core = lax.axis_index("sec")

    @pl.when(core == 0)
    def _():
        across[...] = across_0[...]
        inside[...] = inside_0[...]
        own[...] = own_0[...]
        ocean[...] = other[...]

    @pl.when(core == 1)
    def _():
        remap(slots, other, weights, across, inside, own, *scratch)
        ocean[...] = level[...]


def back_kernel(
    slots, inside, across, own, turned, kept, sent, codes, semaphore, tiles, sums
):
    fetch = pltpu.make_async_copy(slots, codes, semaphore)
    fetch.start()
    _, count, fields, width = tiles.shape
    core, distances, found = place()
    for t in range(count):
        span = slice(t * width, (t + 1) * width)
        tiles[0, t] = across[:, span].astype(jnp.float32)
        tiles[1, t] = inside[:, span].astype(jnp.float32)
        tiles[2, t] = own[:, span].astype(jnp.float32)
    sums[...] = jnp.zeros_like(sums)
    fetch.wait()
    for i, (g, p, slot, at) in enumerate(slot_jobs(core, distances, codes.shape[2])):
        code = codes[0, p, slot]
        source = jnp.bitwise_and(lax.shift_right_logical(code, 8), 255)
        part = tiles[g, source].astype(jnp.bfloat16)
        product = jnp.dot(part, turned[at], preferred_element_type=jnp.float32)
        target = jnp.bitwise_and(code, 255)
        keep = lax.shift_right_logical(code, 16) == 1
        if g < 2:
            keep = jnp.logical_and(keep, found[g])
        sums[i % 2, target] = sums[i % 2, target] + jnp.where(keep, product, 0.0)

    @pl.when(core == 0)
    def _():
        for t in range(count):
            kept[:, t * width : (t + 1) * width] = sums[0, t] + sums[1, t]
        sent[...] = jnp.zeros_like(sent)

    @pl.when(core == 1)
    def _():
        for t in range(count):
            sent[:, t * width : (t + 1) * width] = sums[0, t] + sums[1, t]
        kept[...] = own[...].astype(jnp.float32)


def mix_kernel(held, mixing, own, out, head, passed, mixed, semaphore):
    fields, levels, _ = held.shape
    rows = head.shape[1]
    copies = []
    for f in range(fields):
        total = held[f].astype(jnp.float32) + jnp.dot(
            mixing[0, 0], held[f], preferred_element_type=jnp.float32
        )
        head[f] = total[0:rows].astype(jnp.bfloat16)
        mixed[f] = total[rows:].astype(jnp.bfloat16)
        copies.append(
            pltpu.make_async_copy(
                mixed.at[f], out.at[0, 0, f, pl.ds(rows, levels - rows)], semaphore.at[f]
            )
        )
        copies[f].start()
    passed[...] = own[...]
    for copy in copies:
        copy.wait()


def top_kernel(head, level, flux, weights, columns, out, turned, tops, semaphore):
    del columns
    fields, rows, cells = head.shape
    share = jnp.where(lax.axis_index("sec") == 1, step_weight, 0.0)
    top = level[...] + share * flux[...].astype(jnp.float32)
    row = lax.broadcasted_iota(jnp.int32, (rows, cells), 0)
    copies = []
    for f in range(fields):
        above = jnp.broadcast_to(top[f : f + 1, :], (rows, cells))
        tops[f] = jnp.where(row == 0, above, head[f].astype(jnp.float32)).astype(jnp.bfloat16)
        copies.append(
            pltpu.make_async_copy(tops.at[f], out.at[0, 0, f, pl.ds(0, rows)], semaphore.at[f])
        )
        copies[f].start()
    for at in range(weights.shape[0]):
        turned[at] = weights[at].T
    for copy in copies:
        copy.wait()


def local(
    columns, mixing, lagged_flux, coefficients, ocean_mask, atm_tile, ocean_tile, live, weights
):
    _, _, fields, levels, cells = columns.shape
    width = weights.shape[3]
    tiles = cells // width
    count = lax.axis_size("blk")
    codes = atm_tile + 256 * ocean_tile + 65536 * live
    swap = swap_pairs(count)
    lower, across, upper = exchange_pairs(count)
    inside = [a if a[0] % count % 8 < 4 else b for a, b in zip(lower, upper)]
    field_f32 = jax.ShapeDtypeStruct((fields, cells), jnp.float32)
    field_bf16 = jax.ShapeDtypeStruct((fields, cells), jnp.bfloat16)

    slots = weights.shape[2]
    level, held, picked = pl.pallas_call(
        level_kernel,
        out_shape=(
            field_f32,
            jax.ShapeDtypeStruct(columns.shape[2:], jnp.bfloat16),
            jax.ShapeDtypeStruct((5 * slots // 2, width, width), jnp.bfloat16),
        ),
        in_specs=[HBM, HBM, HBM, HBM],
        out_specs=(VMEM, VMEM, VMEM),
        scratch_shapes=[
            pltpu.VMEM((16, levels), jnp.bfloat16),
            pltpu.VMEM((fields, cells), jnp.bfloat16),
            pltpu.SemaphoreType.DMA((fields,)),
            pltpu.SemaphoreType.DMA((2,)),
            pltpu.SemaphoreType.DMA((3,)),
        ],
        compiler_params=pltpu.CompilerParams(vmem_limit_bytes=8 << 20),
    )(*(pltpu.with_memory_space_constraint(x, pltpu.HBM) for x in (columns, mixing, lagged_flux, weights)))
    other_level = lax.ppermute(level, axes, swap)

    scratch = [
        pltpu.SMEM(codes.shape, jnp.int32),
        pltpu.SemaphoreType.DMA,
        pltpu.VMEM((tiles, fields, width), jnp.float32),
        pltpu.VMEM((3, tiles, fields, width), jnp.float32),
    ]
    early = pl.pallas_call(
        first_remap_kernel,
        out_shape=(field_bf16, field_bf16, field_f32),
        in_specs=[VMEM, VMEM, VMEM],
        out_specs=(VMEM,) * 3,
        scratch_shapes=scratch,
        cost_estimate=pl.CostEstimate(
            flops=5 * slots * fields * width * width,
            transcendentals=0,
            bytes_accessed=5 * slots * width * width,
        ),
        compiler_params=pltpu.CompilerParams(vmem_limit_bytes=8 << 20),
    )(codes, level, picked)
    to_across, to_inside, own, ocean_level = pl.pallas_call(
        second_remap_kernel,
        out_shape=(field_bf16, field_bf16, field_f32, field_f32),
        in_specs=[VMEM] * 7,
        out_specs=(VMEM,) * 4,
        scratch_shapes=scratch,
        compiler_params=pltpu.CompilerParams(vmem_limit_bytes=8 << 20),
    )(codes, level, other_level, picked, *early)
    most_columns, head, own = pl.pallas_call(
        mix_kernel,
        out_shape=(
            jax.ShapeDtypeStruct(columns.shape, jnp.bfloat16),
            jax.ShapeDtypeStruct((fields, 16, cells), jnp.bfloat16),
            field_f32,
        ),
        in_specs=[VMEM, VMEM, VMEM],
        out_specs=(HBM, VMEM, VMEM),
        scratch_shapes=[
            pltpu.VMEM((fields, levels - 16, cells), jnp.bfloat16),
            pltpu.SemaphoreType.DMA((fields,)),
        ],
        cost_estimate=pl.CostEstimate(
            flops=2 * fields * levels * levels * cells,
            transcendentals=0,
            bytes_accessed=4 * fields * levels * cells,
        ),
        compiler_params=pltpu.CompilerParams(vmem_limit_bytes=16 << 20),
    )(pltpu.with_memory_space_constraint(held, pltpu.VMEM), mixing, own)
    partial = own
    for part, pairs in ((to_across, across), (to_inside, inside)):
        partial = partial + lax.ppermute(part, axes, pairs).astype(jnp.float32)
    remapped = partial + lax.ppermute(partial, axes, swap)

    difference = remapped - ocean_level
    speed = jnp.sqrt(
        difference[0:1] * difference[0:1] + difference[1:2] * difference[1:2] + 1.0
    )
    ocean_flux = (
        coefficients[:, None] * speed * difference * ocean_mask.astype(jnp.float32)
    ).astype(jnp.bfloat16)
    flux_across = lax.ppermute(ocean_flux, axes, across)
    flux_inside = lax.ppermute(ocean_flux, axes, inside)

    new_columns, turned = pl.pallas_call(
        top_kernel,
        out_shape=(
            jax.ShapeDtypeStruct(columns.shape, jnp.bfloat16),
            jax.ShapeDtypeStruct(picked.shape, jnp.bfloat16),
        ),
        in_specs=[VMEM, VMEM, VMEM, VMEM, HBM],
        out_specs=(HBM, VMEM),
        input_output_aliases={4: 0},
        scratch_shapes=[
            pltpu.VMEM((fields, 16, cells), jnp.bfloat16),
            pltpu.SemaphoreType.DMA((fields,)),
        ],
        compiler_params=pltpu.CompilerParams(vmem_limit_bytes=8 << 20),
    )(head, level, ocean_flux, picked, most_columns)

    kept, sent = pl.pallas_call(
        back_kernel,
        out_shape=(field_f32, field_f32),
        in_specs=[VMEM, VMEM, VMEM, VMEM, VMEM],
        out_specs=(VMEM, VMEM),
        scratch_shapes=[
            pltpu.SMEM(codes.shape, jnp.int32),
            pltpu.SemaphoreType.DMA,
            pltpu.VMEM((3, tiles, fields, width), jnp.float32),
            pltpu.VMEM((2, tiles, fields, width), jnp.float32),
        ],
        compiler_params=pltpu.CompilerParams(vmem_limit_bytes=8 << 20),
    )(codes, flux_inside, flux_across, ocean_flux, turned)
    flux_here = (kept + lax.ppermute(sent, axes, swap)).astype(jnp.bfloat16)
    return (new_columns, flux_here[None, None])


def solution(mesh):
    in_specs = (
        P("sec", "blk", None, None, None),
        P("sec", "blk", None, None),
        P("blk", None, None),
        P(),
        P("blk", None),
        P("blk", None, None),
        P("blk", None, None),
        P("blk", None, None),
        P("blk", None, None, None, None),
    )
    out_specs = (P("sec", "blk", None, None, None), P("sec", "blk", None, None))
    return jax.shard_map(local, mesh=mesh, in_specs=in_specs, out_specs=out_specs, check_vma=False)
```
